512 devices in a mesh: row: 16 (over z, core), sector: 32 (over x, y).
Axes of the slice: x: 4, y: 8, z: 8, core: 2. Of those that a mesh axis runs over, the one named last changes fastest.
Arguments:
- boundary_in: float32 [32, 128, 256], P('sector'), may hold values from -6 to 6
- left_transfer: float32 [16, 32, 128, 128], P('row', 'sector'), may hold values from -0.25 to 0.25
- right_transfer: float32 [16, 256, 256], P('row'), may hold values from -0.36 to 0.36
- env_weight: bfloat16 [16, 16, 256, 256], P('row'), may hold values from -50000 to 50000
- ranks: int32 [32], P('sector'), may hold values from 32 to 128, as said below
- routes: int32 [32, 16], P('sector'), may hold values from 0 to 31, all different within a row; in each aligned block of 32 rows (0 to 31, 32 to 63, ...) at most 24 rows name the same one
- owner: int32 [32], replicated, may hold values from 0 to 31, each once
Outputs:
- boundary_out: float32 [16, 32, 128, 256], P('row', 'sector')
- environment: float32 [16, 32, 128, 256], P('row', 'sector')
The draws below stay inside these ranges and needn't reach their ends.
Inputs may be any that keep to these rules, and one draw needn't show every extreme that they name: `ranks`: at least one sector has rank 128. `routes`: each row names 16 different sectors; no sector is named by more than 24 rows. `owner`: each sector index once.
All inputs are finite; a program needn't handle non-finite values.
Results may differ from the reference program's by a relative error of at most 0.013.
Values may be sent and summed in bfloat16 or wider, within the bound.
No kernel may reach another device: no remote copies, remote signals or barrier semaphores. Data moves between devices by JAX's collectives and lax.ppermute only.
A program may use at most 64 MiB of HBM per device.

```python
import math
import jax
import jax.numpy as jnp
import numpy as np
from jax import lax

PAD = 128
D2 = 256
SLOTS = 16
CAP = 24
SECTORS = 32
ROWS = 16


def draw_ranks(key, part):
    values = jax.random.randint(key, (SECTORS,), PAD // 4, PAD + 1)
    position = jax.random.randint(jax.random.fold_in(key, 7), (), 0, SECTORS)
    return jnp.where(jnp.arange(SECTORS) == position, PAD, values).astype(jnp.int32)


def draw_boundary_in(key, part):
    values = jax.random.truncated_normal(key, -6.0, 6.0, (SECTORS, PAD, D2), jnp.float32)
    return values.astype(jnp.float32)


def draw_right_transfer(key, part):
    sigma = 0.5 / jnp.sqrt(jnp.float32(D2))
    values = jax.random.truncated_normal(key, -4.0, 4.0, (ROWS, D2, D2), jnp.float32) * sigma
    values = jnp.clip(values, -0.36, 0.36)
    return values.astype(jnp.float32)


def draw_env_weight(key, part):
    values = jax.random.truncated_normal(key, -4.0, 4.0, (ROWS, SLOTS, D2, D2), jnp.float32)
    values = values / jnp.sqrt(jnp.float32(D2))
    return values.astype(jnp.bfloat16)


def levels(own_key, extent, cuts, least, top_value):
    factor_of, own = 1.0, jax.random.fold_in(own_key, 6)
    for dim, parts in cuts:
        heights = jnp.exp(jax.random.uniform(jax.random.fold_in(own, dim), (parts,), jnp.float32, least / len(cuts), top_value / len(cuts)))
        factor_of = factor_of * jnp.repeat(heights, extent[dim] // parts).reshape([-1 if axis == dim else 1 for axis in range(len(extent))])
    return factor_of


def shared_out(stream_key, own, number, rows, amount, top, most, lean):
    order = jax.random.permutation(stream_key, amount)
    packed, usual = load_shares(amount, rows * top, most, lean, True), load_shares(amount, rows * top, most, lean, False)
    places = jnp.arange(amount)

    def named(sizes, offset_by):
        used = int((sizes > 0).sum())
        fixed = max(1, used // 4)
        shifted = fixed + (places - fixed + offset_by * (used - fixed)) % max(1, amount - fixed)
        return jnp.zeros((amount,), jnp.int32).at[order[jnp.where(places < fixed, places, shifted)]].set(jnp.asarray(sizes, jnp.int32))

    sizes = jnp.where(number % 4 == 0, named(packed, number // 4), named(usual, number - number // 4 - 1))
    mixed = jax.random.permutation(jax.random.fold_in(own, 3), amount)
    source_of, taker = mixed[0:amount // 2 * 2:2], mixed[1:amount // 2 * 2:2]
    slack = jnp.minimum(sizes[source_of] - 1, most - sizes[taker]) // 2
    slack = jnp.where((source_of == order[0]) | (taker == order[0]) | (sizes[taker] == 0), 0, jnp.maximum(slack, 0))
    shifted = jax.random.randint(jax.random.fold_in(own, 4), (amount // 2,), 0, 1 << 20) % (slack + 1)
    sizes = sizes.at[source_of].add(-shifted).at[taker].add(shifted)
    labels = jnp.searchsorted(jnp.cumsum(sizes), jnp.arange(rows * top), side="right").astype(jnp.int32)
    listing = labels.reshape(top, rows).T
    listing = listing[jax.random.permutation(jax.random.fold_in(own, 1), rows)]
    offset_by = jax.random.randint(jax.random.fold_in(own, 2), (rows, 1), 0, top)
    return jnp.take_along_axis(listing, (jnp.arange(top)[None, :] + offset_by) % top, axis=1)


def load_shares(number_of, total, limit, slope, full):
    loads = [(1 << 20) // math.isqrt(standing ** slope) + 1 for standing in range(1, number_of + 1)]
    largest = limit if full else min(limit, max(-(-total // number_of), total * loads[0] // sum(loads)))
    least = 1 if total - largest >= number_of - 1 else 0
    counts, rest = [largest] + [least] * (number_of - 1), total - largest - least * (number_of - 1)
    while rest > 0:
        free = [i for i in range(1, number_of) if counts[i] < largest] or [i for i in range(1, number_of) if counts[i] < limit]
        whole, left = sum([loads[i] for i in free]), rest
        for i in free:
            more = min(limit - counts[i], max(1, left * loads[i] // whole), rest)
            counts[i] = counts[i] + more
            rest = rest - more
    return np.array(counts)


def centred(stream_key, shape, width, bound, pieces=(), kind=jnp.bfloat16):
    result = jax.random.normal(stream_key, shape, jnp.float32) * width
    if len(pieces) > 0:
        result = levels(stream_key, shape, pieces, -0.22, 0.18) * result
    return jnp.clip(result, min=-bound, max=bound).astype(kind)


def setup_inputs(seed: int = 0) -> dict:
    streams_of = jax.random.split(jax.random.key(seed), 8)
    boundary_in = draw_boundary_in(jax.random.fold_in(streams_of[7], 71), 0)
    left_transfer = centred(streams_of[1], (ROWS, SECTORS, PAD, PAD), (4 * PAD) ** -0.5, 0.25, ((0, 16), (1, 32)), jnp.float32)
    right_transfer = draw_right_transfer(jax.random.fold_in(streams_of[7], 71), 0)
    env_weight = draw_env_weight(jax.random.fold_in(streams_of[7], 71), 0)
    ranks = draw_ranks(jax.random.fold_in(streams_of[7], 71), 0)
    routes_keys = jax.random.split(jax.random.fold_in(streams_of[5], 1), SECTORS // SECTORS)
    routes_turns = jax.random.permutation(jax.random.fold_in(streams_of[5], 3), SECTORS // SECTORS)
    routes = jax.vmap(lambda own, number: shared_out(jax.random.fold_in(streams_of[5], 2), own, number, SECTORS, SECTORS, SLOTS, CAP, 2))(routes_keys, routes_turns).reshape((SECTORS, SLOTS))
    owner = jax.random.permutation(streams_of[6], SECTORS).astype(jnp.int32)
    return {"boundary_in": boundary_in, "left_transfer": left_transfer, "right_transfer": right_transfer, "env_weight": env_weight, "ranks": ranks, "routes": routes, "owner": owner}


def reference(boundary_in, left_transfer, right_transfer, env_weight, ranks, routes, owner):
    highest = lax.Precision.HIGHEST
    kept = (jnp.arange(PAD)[None, :] < ranks[:, None]).astype(jnp.float32)
    current = boundary_in * kept[:, :, None]
    unit_block = jnp.eye(PAD, dtype=jnp.float32)
    unit_pairs = jnp.eye(D2, dtype=jnp.float32)
    matches = (routes[:, :, None] == jnp.arange(SECTORS)[None, None, :]).astype(jnp.int32)
    target_owner = jnp.sum(matches * owner[None, None, :], axis=2)
    selector = (target_owner[:, :, None] == jnp.arange(SECTORS)[None, None, :]).astype(jnp.float32)
    bounds = []
    environs = []
    for row_index in range(ROWS):
        left_op = kept[:, :, None] * (0.9 * unit_block + left_transfer[row_index]) * kept[:, None, :]
        right_op = 0.9 * unit_pairs + right_transfer[row_index]
        current = jnp.einsum("sab,sbc->sac", left_op, current, precision=highest)
        current = jnp.einsum("sac,cd->sad", current, right_op, precision=highest)
        bounds.append(current)
        rounded = current.astype(jnp.bfloat16).astype(jnp.float32)
        partials = jnp.einsum("sab,jbc->sjac", rounded, env_weight[row_index].astype(jnp.float32), precision=highest)
        partials = partials.astype(jnp.bfloat16).astype(jnp.float32)
        environs.append(jnp.einsum("sjo,sjac->oac", selector, partials, precision=highest))
    return jnp.stack(bounds), jnp.stack(environs)
```

```python
import functools

import jax
import jax.numpy as jnp
from jax import lax
from jax.experimental import pallas as pl
from jax.experimental.pallas import tpu as pltpu
from jax.sharding import PartitionSpec as P

CORES = 2
ACROSS = 4


def environment_sums(slots, blocks, weights, targets):
    sources, rows, inner = blocks.shape
    columns = weights.shape[2]

    def kernel(slots_ref, blocks_ref, weights_ref, sums_ref):
        def one_target(target, carried):
            total = jnp.zeros((rows, columns), jnp.float32)
            for source in range(sources):
                slot = slots_ref[source * targets + target]
                block = blocks_ref[source]
                block = jnp.where(slot >= 0, block, jnp.zeros_like(block))
                total += jnp.dot(
                    block,
                    weights_ref[jnp.maximum(slot, 0)],
                    preferred_element_type=jnp.float32,
                )
            sums_ref[target] = total.astype(jnp.bfloat16)
            return carried

        lax.fori_loop(0, targets, one_target, 0)

    return pl.pallas_call(
        kernel,
        out_shape=jax.ShapeDtypeStruct((targets, rows, columns), jnp.bfloat16),
        in_specs=[
            pl.BlockSpec(memory_space=pltpu.SMEM),
            pl.BlockSpec(memory_space=pltpu.VMEM),
            pl.BlockSpec(memory_space=pltpu.VMEM),
        ],
        out_specs=pl.BlockSpec(memory_space=pltpu.VMEM),
        cost_estimate=pl.CostEstimate(
            flops=2 * sources * targets * rows * inner * columns,
            bytes_accessed=2 * (blocks.size + weights.size + targets * rows * columns),
            transcendentals=0,
        ),
    )(slots, blocks, weights)


def on_device(boundary_in, left_transfer, right_transfer, env_weight, ranks, routes, owner):
    highest = lax.Precision.HIGHEST
    block_size = boundary_in.shape[1]
    pair_size = boundary_in.shape[2]
    row_count = lax.axis_size("row")
    sector_count = lax.axis_size("sector")
    along = sector_count // ACROSS
    same_y = [[x * along + y for x in range(ACROSS)] for y in range(along)]
    same_x = [[x * along + y for y in range(along)] for x in range(ACROSS)]
    row_position = lax.axis_index("row")
    sector_position = lax.axis_index("sector")

    shared_routes = lax.all_to_all(
        jnp.broadcast_to(routes, (ACROSS, routes.shape[1])),
        "sector", 0, 0, axis_index_groups=same_y, tiled=True,
    )
    sector_ids = jnp.arange(sector_count)
    matches = (shared_routes[:, :, None] == sector_ids[None, None, :]).astype(jnp.int32)
    target_owner = jnp.sum(matches * owner[None, None, :], axis=2)
    line = (sector_position // along) * along + jnp.arange(along)
    hits = (target_owner[:, None, :] == line[None, :, None]).astype(jnp.int32)
    slot_ids = jnp.arange(routes.shape[1]) + 1
    slots = (jnp.sum(hits * slot_ids[None, None, :], axis=2) - 1).reshape(-1)

    kept_rows = (jnp.arange(block_size) < ranks[0]).astype(jnp.float32)
    initial = boundary_in[0] * kept_rows[:, None]
    unit_block = jnp.eye(block_size, dtype=jnp.float32)
    unit_pairs = jnp.eye(pair_size, dtype=jnp.float32)

    def left_of(transfer):
        return kept_rows[:, None] * (0.9 * unit_block + transfer) * kept_rows[None, :]

    def right_of(transfer):
        return 0.9 * unit_pairs + transfer

    def times(a, b):
        return jnp.dot(a, b, precision=highest, preferred_element_type=jnp.float32)

    left_op = left_of(left_transfer[0, 0])
    right_op = right_of(right_transfer[0])
    before = [(row, row + 1) for row in range(CORES - 1, row_count - 1, CORES)]
    left_before = left_of(lax.ppermute(left_transfer[0, 0], "row", before))
    right_before = right_of(lax.ppermute(right_transfer[0], "row", before))
    left_two = times(left_op, left_before)
    right_two = times(right_before, right_op)

    current = times(times(left_op, initial), right_op)
    for row in range(0, row_count - CORES, CORES):
        arrived = lax.ppermute(current, "row", [(row, row + CORES)])
        current = jnp.where(
            row_position == row + CORES, times(times(left_two, arrived), right_two), current
        )
    inside = [(row, row + 1) for row in range(0, row_count, CORES)]
    handed = lax.ppermute(current, "row", inside)
    current = jnp.where(
        row_position % CORES == 0, current, times(times(left_op, handed), right_op)
    )

    rounded = current.astype(jnp.bfloat16)
    blocks = lax.all_to_all(
        jnp.broadcast_to(rounded, (ACROSS,) + rounded.shape),
        "sector", 0, 0, axis_index_groups=same_y, tiled=True,
    )
    sums = environment_sums(slots, blocks, env_weight[0], along)
    terms = lax.all_to_all(sums, "sector", 0, 0, axis_index_groups=same_x, tiled=True)
    environment = jnp.sum(terms.astype(jnp.float32), axis=0)
    return (current[None, None], environment[None, None])


def solution(mesh):
    return jax.shard_map(
        on_device,
        mesh=mesh,
        in_specs=(
            P("sector", None, None),
            P("row", "sector", None, None),
            P("row", None, None),
            P("row", None, None, None),
            P("sector"),
            P("sector", None),
            P(),
        ),
        out_specs=(P("row", "sector", None, None), P("row", "sector", None, None)),
        check_vma=False,
    )
```

```python
import jax
import jax.numpy as jnp
from jax import lax
from jax.experimental import pallas as pl
from jax.experimental.pallas import tpu as pltpu
from jax.sharding import PartitionSpec as P

PIECE_ROWS = 8
PIECE_COLUMNS = 128


def environment_pieces(arrived, weights):
    slots, inner, columns = weights.shape
    sectors = arrived.shape[0]
    count = sectors * PIECE_ROWS

    def kernel(arrived_ref, weights_ref, out_ref):
        pieces = arrived_ref[:, :PIECE_ROWS, :].reshape(count, inner)
        half = lax.rem(lax.axis_index("sector"), columns // PIECE_COLUMNS)
        start = pl.multiple_of(half * PIECE_COLUMNS, PIECE_COLUMNS)
        rows = lax.broadcasted_iota(jnp.int32, (count, count), 0).astype(jnp.float32)
        marks = arrived_ref[:, PIECE_ROWS:, :].astype(jnp.float32)
        first = jnp.sum(marks[: sectors // 2], axis=0)
        second = jnp.sum(marks[sectors // 2 :], axis=0)

        total = jnp.zeros((count, PIECE_COLUMNS), jnp.float32)
        for slot in range(slots):
            partial = jnp.dot(
                pieces,
                weights_ref[slot, :, pl.ds(start, PIECE_COLUMNS)],
                preferred_element_type=jnp.float32,
            ).astype(jnp.bfloat16)
            line, part = slot % PIECE_ROWS, slot // PIECE_ROWS * PIECE_COLUMNS
            lanes = slice(part, part + PIECE_COLUMNS)
            places = jnp.concatenate(
                [first[line : line + 1, lanes], second[line : line + 1, lanes]], axis=1
            )
            place = jnp.where(rows == places, 1.0, 0.0).astype(jnp.bfloat16)
            total += jnp.dot(place, partial, preferred_element_type=jnp.float32)
        out_ref[...] = total

    return pl.pallas_call(
        kernel,
        out_shape=jax.ShapeDtypeStruct((count, PIECE_COLUMNS), jnp.float32),
        in_specs=[
            pl.BlockSpec(memory_space=pltpu.VMEM),
            pl.BlockSpec(memory_space=pltpu.VMEM),
        ],
        out_specs=pl.BlockSpec(memory_space=pltpu.VMEM),
        compiler_params=pltpu.CompilerParams(vmem_limit_bytes=8 * 1024 * 1024),
        cost_estimate=pl.CostEstimate(
            flops=4 * slots * count * inner * PIECE_COLUMNS,
            bytes_accessed=2 * weights.size + 8 * count * inner,
            transcendentals=0,
        ),
    )(arrived, weights)


def on_device(boundary_in, left_transfer, right_transfer, env_weight, ranks, routes, owner):
    highest = lax.Precision.HIGHEST
    block_size = boundary_in.shape[1]
    pair_size = boundary_in.shape[2]
    slot_count = routes.shape[1]
    row_count = lax.axis_size("row")
    sector_count = lax.axis_size("sector")
    row = lax.axis_index("row")
    sector = lax.axis_index("sector")
    kept_rows = (jnp.arange(block_size) < ranks[0]).astype(jnp.float32)
    initial = boundary_in[0] * kept_rows[:, None]
    unit_block = jnp.eye(block_size, dtype=jnp.float32)
    unit_pairs = jnp.eye(pair_size, dtype=jnp.float32)

    def left_of(transfer):
        return kept_rows[:, None] * (0.9 * unit_block + transfer) * kept_rows[None, :]

    def right_of(transfer):
        return 0.9 * unit_pairs + transfer

    def times(a, b):
        return jnp.dot(a, b, precision=highest, preferred_element_type=jnp.float32)

    def absorb(left, block, right):
        return times(times(left, block), right)

    def sent(value, pairs):
        return lax.ppermute(value, "row", pairs)

    left_op = left_of(left_transfer[0, 0])
    right_op = right_of(right_transfer[0])
    to_second = [(r, r + 1) for r in range(0, row_count, 2)]
    left_low = left_of(sent(left_transfer[0, 0], to_second))
    right_low = right_of(sent(right_transfer[0], to_second))
    left_two = times(left_op, left_low)
    right_two = times(right_low, right_op)

    current = absorb(left_two, initial, right_two)
    next_chip = [(r, r + 2) for r in range(5, row_count, 4)]
    arrived = sent(current, [(1, 3)])
    left_half = sent(left_two, next_chip)
    right_half = sent(right_two, next_chip)
    source = jnp.where(row == 3, arrived, initial)
    current = jnp.where(row == 3, absorb(left_two, arrived, right_two), current)

    left_four = times(left_two, left_half)
    right_four = times(right_half, right_two)
    for last in range(3, row_count - 4, 4):
        arrived = sent(current, [(last, last + 4)])
        source = jnp.where(row == last + 4, arrived, source)
        current = jnp.where(row == last + 4, absorb(left_four, arrived, right_four), current)

    to_first = [(r + 1, r) for r in range(2, row_count, 2)]
    left_relay = sent(left_half, to_first[2::2])
    right_relay = sent(right_half, to_first[2::2])
    arrived = sent(current, [(r, r + 2) for r in range(3, row_count - 2, 4)])
    source = jnp.where((row % 4 == 1) & (row > 1), arrived, source)
    arrived = sent(source, to_first)
    source = jnp.where((row % 2 == 0) & (row > 0), arrived, source)
    second = row % 2 == 1
    joined = (row % 4 == 2) & (row > 4)
    left_own = jnp.where(second, left_two, left_op)
    right_own = jnp.where(second, right_two, right_op)
    left_own = jnp.where(joined, times(left_op, left_relay), left_own)
    right_own = jnp.where(joined, times(right_relay, right_op), right_own)
    current = jnp.where(row % 4 == 3, current, absorb(left_own, source, right_own))

    sector_ids = jnp.arange(sector_count)
    matches = (routes[0][:, None] == sector_ids[None, :]).astype(jnp.int32)
    target_owner = jnp.sum(matches * owner[None, :], axis=1)
    halves = pair_size // PIECE_COLUMNS
    cuts = block_size // PIECE_ROWS
    lane = jnp.arange(PIECE_COLUMNS)
    places = target_owner[:, None] * PIECE_ROWS + (lane % PIECE_ROWS)[None, :]
    places = jnp.where(lane // PIECE_ROWS == sector % cuts, places, 0).astype(jnp.bfloat16)
    marks = places.reshape(slot_count // PIECE_ROWS, PIECE_ROWS, PIECE_COLUMNS)
    marks = marks.transpose(1, 0, 2).reshape(1, PIECE_ROWS, pair_size)
    rounded = current.astype(jnp.bfloat16).reshape(cuts, PIECE_ROWS, pair_size)
    outgoing = jnp.concatenate([rounded, jnp.broadcast_to(marks, rounded.shape)], axis=1)
    outgoing = jnp.broadcast_to(outgoing[:, None], (cuts, halves) + outgoing.shape[1:])
    pieces = lax.all_to_all(
        outgoing.reshape(sector_count, 2 * PIECE_ROWS, pair_size), "sector", 0, 0, tiled=True
    )
    sums = environment_pieces(pieces, env_weight[0])
    back = lax.all_to_all(
        sums.reshape(sector_count, PIECE_ROWS, PIECE_COLUMNS), "sector", 0, 0, tiled=True
    )
    environment = back.reshape(cuts, halves, PIECE_ROWS, PIECE_COLUMNS)
    environment = environment.transpose(0, 2, 1, 3).reshape(block_size, pair_size)
    return (current[None, None], environment[None, None])


def solution(mesh):
    return jax.shard_map(
        on_device,
        mesh=mesh,
        in_specs=(
            P("sector", None, None),
            P("row", "sector", None, None),
            P("row", None, None),
            P("row", None, None, None),
            P("sector"),
            P("sector", None),
            P(),
        ),
        out_specs=(P("row", "sector", None, None), P("row", "sector", None, None)),
        check_vma=False,
    )
```

```python
import jax
import jax.numpy as jnp
from jax import lax
from jax.experimental import pallas as pl
from jax.experimental.pallas import tpu as pltpu
from jax.sharding import PartitionSpec as P

ALONG = 8
PAIR = 2
EXTRA = 8
VMEM_GRANT = 8 * 1024 * 1024
HIGHEST = lax.Precision.HIGHEST


def whole(space):
    return pl.BlockSpec(memory_space=space)


def times(a, b):
    return jnp.dot(a, b, precision=HIGHEST, preferred_element_type=jnp.float32)


def absorb(left, block, right):
    return times(times(left, block), right)


def packed(left, right):
    half = left.shape[0] // 2
    return jnp.concatenate([right, jnp.concatenate([left[:half], left[half:]], axis=1)], axis=0)


def unpacked(ref):
    pairs = ref.shape[1]
    size = pairs // 2
    below = ref[pairs:, :]
    return jnp.concatenate([below[:, :size], below[:, size:]], axis=0), ref[:pairs, :]


def store_packed(ref, left, right):
    pairs = ref.shape[1]
    half = left.shape[0] // 2
    ref[:pairs, :] = right
    ref[pairs:, : pairs // 2] = left[:half]
    ref[pairs:, pairs // 2 :] = left[half:]


def on_core(kernel, shapes, *operands, scalar=False):
    spaces = [pltpu.VMEM] * len(operands)
    if scalar:
        spaces[0] = pltpu.SMEM
    moved = sum(4 * operand.size for operand in operands)
    return pl.pallas_call(
        kernel,
        out_shape=shapes,
        in_specs=[whole(space) for space in spaces],
        out_specs=[whole(pltpu.VMEM)] * len(shapes),
        compiler_params=pltpu.CompilerParams(vmem_limit_bytes=VMEM_GRANT),
        cost_estimate=pl.CostEstimate(
            flops=256 * moved, bytes_accessed=2 * moved, transcendentals=0
        ),
    )(*operands)


def like(array):
    return jax.ShapeDtypeStruct(array.shape, jnp.float32)


def operators(rank, initial, own, low):
    def kernel(rank_ref, block_ref, own_ref, low_ref, own_out, two_out, block_out):
        rank = rank_ref[0]

        def whole_of(ref):
            left, right = unpacked(ref)
            rows = lax.broadcasted_iota(jnp.int32, left.shape, 0)
            columns = lax.broadcasted_iota(jnp.int32, left.shape, 1)
            kept = jnp.logical_and(rows < rank, columns < rank)
            left = jnp.where(kept, left + jnp.where(rows == columns, 0.9, 0.0), 0.0)
            rows = lax.broadcasted_iota(jnp.int32, right.shape, 0)
            columns = lax.broadcasted_iota(jnp.int32, right.shape, 1)
            return left, right + jnp.where(rows == columns, 0.9, 0.0)

        left, right = whole_of(own_ref)
        store_packed(own_out, left, right)
        left_low, right_low = whole_of(low_ref)
        left, right = times(left, left_low), times(right_low, right)
        store_packed(two_out, left, right)
        block_out[...] = absorb(left, block_ref[...], right)

    shapes = [like(own), like(own), like(initial)]
    return on_core(kernel, shapes, rank, initial, own, low, scalar=True)


def joined(later, earlier):
    def kernel(later_ref, earlier_ref, out_ref):
        left, right = unpacked(later_ref)
        left_before, right_before = unpacked(earlier_ref)
        store_packed(out_ref, times(left, left_before), times(right_before, right))

    return on_core(kernel, [like(later)], later, earlier)[0]


def taken(operator, block):
    def kernel(operator_ref, block_ref, out_ref):
        left, right = unpacked(operator_ref)
        out_ref[...] = absorb(left, block_ref[...], right)

    return on_core(kernel, [like(block)], operator, block)[0]


def last_rows(copies, operator, block, extra):
    rows, columns = block.shape

    def kernel(operator_ref, block_ref, extra_ref, block_out, outgoing_ref):
        left, right = unpacked(operator_ref)
        own = absorb(left, block_ref[...], right)
        block_out[...] = own
        rounded = own.astype(jnp.bfloat16)
        for index in range(copies):
            outgoing_ref[index, :rows, :] = rounded
            outgoing_ref[index, rows:, :] = extra_ref[...]

    outgoing = jax.ShapeDtypeStruct((copies, rows + EXTRA, columns), jnp.bfloat16)
    return on_core(kernel, [like(block), outgoing], operator, block, extra)


def environment_sums(slots, arrived, weights):
    sources, targets = slots.shape
    slot_count, inner, columns = weights.shape
    rows = arrived.shape[1] - EXTRA

    def kernel(slots_ref, arrived_ref, weights_ref, sums_ref):
        def one_target(target, carried):
            total = jnp.zeros((rows, columns), jnp.float32)
            for source in range(sources):
                slot = slots_ref[source, target]
                block = arrived_ref[source, :rows, :]
                block = jnp.where(slot >= 0, block, jnp.zeros_like(block))
                slot = jnp.minimum(jnp.maximum(slot, 0), slot_count - 1)
                total += jnp.dot(block, weights_ref[slot], preferred_element_type=jnp.float32)
            sums_ref[target] = total.astype(jnp.bfloat16)
            return carried

        lax.fori_loop(0, targets, one_target, 0)

    return pl.pallas_call(
        kernel,
        out_shape=jax.ShapeDtypeStruct((targets, rows, columns), jnp.bfloat16),
        in_specs=[whole(pltpu.SMEM), whole(pltpu.VMEM), whole(pltpu.VMEM)],
        out_specs=whole(pltpu.VMEM),
        compiler_params=pltpu.CompilerParams(vmem_limit_bytes=VMEM_GRANT),
        cost_estimate=pl.CostEstimate(
            flops=2 * sources * targets * rows * inner * columns,
            bytes_accessed=2 * (arrived.size + weights.size + targets * rows * columns),
            transcendentals=0,
        ),
    )(slots, arrived, weights)


def on_device(boundary_in, left_transfer, right_transfer, env_weight, ranks, routes, owner):
    block_size = boundary_in.shape[1]
    row_count = lax.axis_size("row")
    sector_count = lax.axis_size("sector")
    row = lax.axis_index("row")
    sector = lax.axis_index("sector")

    def sent(value, pairs):
        return lax.ppermute(value, "row", pairs)

    kept_rows = (jnp.arange(block_size) < ranks[0]).astype(jnp.float32)
    initial = boundary_in[0] * kept_rows[:, None]
    raw = packed(left_transfer[0, 0], right_transfer[0])
    low = sent(raw, [(r, r + 1) for r in range(0, row_count, 2)])
    own, two, block = operators(ranks, initial, raw, low)
    arrived = sent(block, [(1, 3)])
    half = sent(two, [(r, r + 2) for r in range(5, row_count, 4)])

    source = jnp.where(row == 3, arrived, initial)
    block = taken(two, arrived)
    leaving = block
    four = joined(two, half)
    hops = list(range(3, row_count - 4, 4))
    for last in hops:
        arrived = sent(block, [(last, last + 4)])
        source = jnp.where(row == last + 4, arrived, source)
        if last != hops[-1]:
            block = taken(four, arrived)
            leaving = jnp.where(row == last + 4, block, leaving)

    arrived = sent(leaving, [(r, r + 2) for r in range(3, row_count - 2, 4)])
    to_first = [(r + 1, r) for r in range(2, row_count, 2)]
    relayed = sent(half, to_first[2::2])
    source = jnp.where((row % 4 == 1) & (row > 1), arrived, source)
    arrived = sent(source, to_first)
    source = jnp.where((row % 2 == 0) & (row > 0), arrived, source)
    second = row % 2 == 1
    base = jnp.where(second, two, own)
    final = joined(base, jnp.where(second, half, relayed))
    final = jnp.where((row % 4 >= 2) & (row >= 4), final, base)

    along = ALONG
    across = sector_count // along
    parts = along // PAIR
    tiles = [
        [x * along + part * PAIR + y for x in range(across) for y in range(PAIR)]
        for part in range(parts)
    ]
    lines = [
        [x * along + part * PAIR + y for part in range(parts)]
        for x in range(across)
        for y in range(PAIR)
    ]
    sector_ids = jnp.arange(sector_count)
    matches = (routes[0][:, None] == sector_ids[None, :]).astype(jnp.int32)
    target_owner = jnp.sum(matches * owner[None, :], axis=1)
    hits = (target_owner[:, None] == jnp.arange(block_size * 2)[None, :]).astype(jnp.int32)
    slot_of = jnp.sum(hits * (jnp.arange(routes.shape[1]) + 1)[:, None], axis=0)
    extra = jnp.broadcast_to(slot_of.astype(jnp.bfloat16), (EXTRA, block_size * 2))
    current, outgoing = last_rows(across * PAIR, final, source, extra)
    arrived = lax.all_to_all(
        outgoing,
        "sector", 0, 0, axis_index_groups=tiles, tiled=True,
    )
    targets = (sector // along) * along + sector % PAIR + jnp.arange(parts) * PAIR
    wanted = (jnp.arange(block_size * 2)[None, :] == targets[:, None]).astype(jnp.float32)
    slots = jnp.sum(arrived[:, block_size, None, :].astype(jnp.float32) * wanted[None], axis=2)
    sums = environment_sums(slots.astype(jnp.int32) - 1, arrived, env_weight[0])
    terms = lax.all_to_all(sums, "sector", 0, 0, axis_index_groups=lines, tiled=True)
    environment = jnp.sum(terms.astype(jnp.float32), axis=0)
    return (current[None, None], environment[None, None])


def solution(mesh):
    return jax.shard_map(
        on_device,
        mesh=mesh,
        in_specs=(
            P("sector", None, None),
            P("row", "sector", None, None),
            P("row", None, None),
            P("row", None, None, None),
            P("sector"),
            P("sector", None),
            P(),
        ),
        out_specs=(P("row", "sector", None, None), P("row", "sector", None, None)),
        check_vma=False,
    )
```

```python
import jax
import jax.numpy as jnp
from jax import lax
from jax.experimental import pallas as pl
from jax.experimental.pallas import tpu as pltpu
from jax.sharding import PartitionSpec as P

ALONG = 8
PAIR = 2
EXTRA = 8
VMEM_GRANT = 8 * 1024 * 1024


def whole(space):
    return pl.BlockSpec(memory_space=space)


def times(a, b):
    def parts(value):
        head = value.astype(jnp.bfloat16)
        return head, (value - head.astype(jnp.float32)).astype(jnp.bfloat16)

    def dot(first, second):
        return jnp.dot(first, second, preferred_element_type=jnp.float32)

    (a_head, a_rest), (b_head, b_rest) = parts(a), parts(b)
    return dot(a_head, b_head) + (dot(a_head, b_rest) + dot(a_rest, b_head))


def absorb(left, block, right):
    return times(times(left, block), right)


def unpacked(ref):
    pairs = ref.shape[1]
    size = pairs // 2
    below = ref[pairs:, :]
    return jnp.concatenate([below[:, :size], below[:, size:]], axis=0), ref[:pairs, :]


def store_packed(ref, left, right):
    pairs = ref.shape[1]
    half = left.shape[0] // 2
    ref[:pairs, :] = right
    ref[pairs:, : pairs // 2] = left[:half]
    ref[pairs:, pairs // 2 :] = left[half:]


def on_core(kernel, shapes, *operands, scalar=False):
    spaces = [pltpu.VMEM] * len(operands)
    if scalar:
        spaces[0] = pltpu.SMEM
    moved = sum(4 * operand.size for operand in operands)
    return pl.pallas_call(
        kernel,
        out_shape=shapes,
        in_specs=[whole(space) for space in spaces],
        out_specs=[whole(pltpu.VMEM)] * len(shapes),
        compiler_params=pltpu.CompilerParams(vmem_limit_bytes=VMEM_GRANT),
        cost_estimate=pl.CostEstimate(
            flops=256 * moved, bytes_accessed=2 * moved, transcendentals=0
        ),
    )(*operands)


def like(array):
    return jax.ShapeDtypeStruct(array.shape, jnp.float32)


def operators(rank, stacked, left_low, right_low):
    size, pairs = left_low.shape[0], right_low.shape[0]

    def kernel(rank_ref, stacked_ref, left_low_ref, right_low_ref, *outs):
        own_out, two_out, kept_out, block_out = outs
        rank = rank_ref[0]
        rows = lax.broadcasted_iota(jnp.int32, (size, size), 0)
        columns = lax.broadcasted_iota(jnp.int32, (size, size), 1)
        kept = jnp.logical_and(rows < rank, columns < rank)
        unit = jnp.where(rows == columns, 0.9, 0.0).astype(jnp.float32)
        left = jnp.where(kept, unit + stacked_ref[size + pairs :, :size], 0.0)
        left_before = jnp.where(kept, unit + left_low_ref[...], 0.0)
        rows = lax.broadcasted_iota(jnp.int32, (pairs, pairs), 0)
        columns = lax.broadcasted_iota(jnp.int32, (pairs, pairs), 1)
        unit = jnp.where(rows == columns, 0.9, 0.0).astype(jnp.float32)
        right = unit + stacked_ref[size : size + pairs, :]
        store_packed(own_out, left, right)
        left, right = times(left, left_before), times(unit + right_low_ref[...], right)
        store_packed(two_out, left, right)
        rows = lax.broadcasted_iota(jnp.int32, (size, pairs), 0)
        kept = jnp.where(rows < rank, stacked_ref[:size, :], 0.0)
        kept_out[...] = kept
        block_out[...] = absorb(left, kept, right)

    packed = jax.ShapeDtypeStruct((pairs + size // 2, pairs), jnp.float32)
    block = jax.ShapeDtypeStruct((size, pairs), jnp.float32)
    operands = rank, stacked, left_low, right_low
    return on_core(kernel, [packed, packed, block, block], *operands, scalar=True)


def joined(later, earlier):
    def kernel(later_ref, earlier_ref, out_ref):
        left, right = unpacked(later_ref)
        left_before, right_before = unpacked(earlier_ref)
        store_packed(out_ref, times(left, left_before), times(right_before, right))

    return on_core(kernel, [like(later)], later, earlier)[0]


def taken(operator, block, copies=1):
    def kernel(operator_ref, block_ref, *outs):
        left, right = unpacked(operator_ref)
        result = absorb(left, block_ref[...], right)
        for out_ref in outs:
            out_ref[...] = result

    return on_core(kernel, [like(block)] * copies, operator, block)


def last_rows(copies, operator, block, extra):
    rows, columns = block.shape

    def kernel(operator_ref, block_ref, extra_ref, block_out, outgoing_ref):
        left, right = unpacked(operator_ref)
        own = absorb(left, block_ref[...], right)
        block_out[...] = own
        rounded = own.astype(jnp.bfloat16)
        for index in range(copies):
            outgoing_ref[index, :rows, :] = rounded
            outgoing_ref[index, rows:, :] = extra_ref[...]

    outgoing = jax.ShapeDtypeStruct((copies, rows + EXTRA, columns), jnp.bfloat16)
    return on_core(kernel, [like(block), outgoing], operator, block, extra)


def environment_sums(slots, arrived, weights):
    sources, targets = slots.shape
    slot_count, inner, columns = weights.shape
    rows = arrived.shape[1] - EXTRA

    def kernel(slots_ref, arrived_ref, weights_ref, sums_ref):
        def one_target(target, carried):
            total = jnp.zeros((rows, columns), jnp.float32)
            for source in range(sources):
                slot = slots_ref[source, target]
                block = arrived_ref[source, :rows, :]
                block = jnp.where(slot >= 0, block, jnp.zeros_like(block))
                slot = jnp.minimum(jnp.maximum(slot, 0), slot_count - 1)
                total += jnp.dot(block, weights_ref[slot], preferred_element_type=jnp.float32)
            sums_ref[target] = total.astype(jnp.bfloat16)
            return carried

        lax.fori_loop(0, targets, one_target, 0)

    return pl.pallas_call(
        kernel,
        out_shape=jax.ShapeDtypeStruct((targets, rows, columns), jnp.bfloat16),
        in_specs=[whole(pltpu.SMEM), whole(pltpu.VMEM), whole(pltpu.VMEM)],
        out_specs=whole(pltpu.VMEM),
        compiler_params=pltpu.CompilerParams(vmem_limit_bytes=VMEM_GRANT),
        cost_estimate=pl.CostEstimate(
            flops=2 * sources * targets * rows * inner * columns,
            bytes_accessed=2 * (arrived.size + weights.size + targets * rows * columns),
            transcendentals=0,
        ),
    )(slots, arrived, weights)


def on_device(boundary_in, left_transfer, right_transfer, env_weight, ranks, routes, owner):
    block_size = boundary_in.shape[1]
    row_count = lax.axis_size("row")
    sector_count = lax.axis_size("sector")
    row = lax.axis_index("row")
    sector = lax.axis_index("sector")

    def sent(value, pairs):
        return lax.ppermute(value, "row", pairs)

    swap = [(r, r + 1) for r in range(0, row_count, 2)]
    right_low = sent(right_transfer[0], swap)
    left_low = sent(left_transfer[0, 0], swap)
    padded = jnp.pad(left_transfer[0, 0], ((0, 0), (0, boundary_in.shape[2] - block_size)))
    stacked = jnp.concatenate([boundary_in[0], right_transfer[0], padded], axis=0)
    own, two, initial, block = operators(ranks, stacked, left_low, right_low)
    arrived = sent(block, [(1, 3)])
    half = sent(two, [(r, r + 2) for r in range(5, row_count, 4)])

    last = row_count - 5
    source = jnp.where(row == 3, arrived, initial)
    (block,) = taken(two, arrived)
    leaving = block
    four = joined(two, half)
    hops = list(range(3, last, 4))
    for hop, start in enumerate(hops):
        arrived = sent(block, [(start, start + 4)])
        source = jnp.where(row == start + 4, arrived, source)
        end = hop == len(hops) - 1
        if end:
            spread = sent(leaving, [(r, r + 2) for r in hops])
            relayed = sent(half, [(r + 1, r) for r in range(6, row_count, 4)])
        block, *more = taken(four, arrived, copies=2 if end else 1)
        if not end:
            leaving = jnp.where(row == start + 4, block, leaving)
    for_end = sent(block, [(last, last + 3)])
    for_spread = sent(more[0], [(last, last + 1)])
    source = jnp.where((row % 4 == 1) & (row > 1), spread, source)
    arrived = sent(source, [(r + 1, r) for r in range(2, last, 2)])
    source = jnp.where((row % 2 == 0) & (row > 0), arrived, source)
    source = jnp.where(row == last + 3, for_end, source)
    source = jnp.where(row == last + 1, for_spread, source)
    arrived = sent(source, [(last + 1, last + 2), (last + 3, last + 4)])
    source = jnp.where((row == last + 2) | (row == last + 4), arrived, source)
    second = row % 2 == 1
    base = jnp.where(second, two, own)
    final = joined(base, jnp.where(second, half, relayed))
    final = jnp.where((row % 4 >= 2) & (row >= 4), final, base)

    along = ALONG
    across = sector_count // along
    parts = along // PAIR
    tiles = [
        [x * along + part * PAIR + y for x in range(across) for y in range(PAIR)]
        for part in range(parts)
    ]
    lines = [
        [x * along + part * PAIR + y for part in range(parts)]
        for x in range(across)
        for y in range(PAIR)
    ]
    sector_ids = jnp.arange(sector_count)
    matches = (routes[0][:, None] == sector_ids[None, :]).astype(jnp.int32)
    target_owner = jnp.sum(matches * owner[None, :], axis=1)
    hits = (target_owner[:, None] == jnp.arange(block_size * 2)[None, :]).astype(jnp.int32)
    slot_of = jnp.sum(hits * (jnp.arange(routes.shape[1]) + 1)[:, None], axis=0)
    extra = jnp.broadcast_to(slot_of.astype(jnp.bfloat16), (EXTRA, block_size * 2))
    current, outgoing = last_rows(across * PAIR, final, source, extra)
    arrived = lax.all_to_all(
        outgoing,
        "sector", 0, 0, axis_index_groups=tiles, tiled=True,
    )
    targets = (sector // along) * along + sector % PAIR + jnp.arange(parts) * PAIR
    wanted = (jnp.arange(block_size * 2)[None, :] == targets[:, None]).astype(jnp.float32)
    slots = jnp.sum(arrived[:, block_size, None, :].astype(jnp.float32) * wanted[None], axis=2)
    sums = environment_sums(slots.astype(jnp.int32) - 1, arrived, env_weight[0])
    terms = lax.all_to_all(sums, "sector", 0, 0, axis_index_groups=lines, tiled=True)
    environment = jnp.sum(terms.astype(jnp.float32), axis=0)
    return (current[None, None], environment[None, None])


def solution(mesh):
    return jax.shard_map(
        on_device,
        mesh=mesh,
        in_specs=(
            P("sector", None, None),
            P("row", "sector", None, None),
            P("row", None, None),
            P("row", None, None, None),
            P("sector"),
            P("sector", None),
            P(),
        ),
        out_specs=(P("row", "sector", None, None), P("row", "sector", None, None)),
        check_vma=False,
    )
```

```python
import jax
import jax.numpy as jnp
from jax import lax
from jax.experimental import pallas as pl
from jax.experimental.pallas import tpu as pltpu
from jax.sharding import PartitionSpec as P

ALONG = 8
PAIR = 2
EXTRA = 8
TILE_ORDER = (2, 3, 0, 1)
LINE_ORDER = (2, 3, 0, 1)
VMEM_GRANT = 8 * 1024 * 1024


def whole(space):
    return pl.BlockSpec(memory_space=space)


def times(a, b):
    def parts(value):
        head = value.astype(jnp.bfloat16)
        return head, (value - head.astype(jnp.float32)).astype(jnp.bfloat16)

    def dot(first, second):
        return jnp.dot(first, second, preferred_element_type=jnp.float32)

    (a_head, a_rest), (b_head, b_rest) = parts(a), parts(b)
    return dot(a_head, b_head) + (dot(a_head, b_rest) + dot(a_rest, b_head))


def absorb(left, block, right):
    return times(times(left, block), right)


def unpacked(ref):
    pairs = ref.shape[1]
    size = pairs // 2
    below = ref[pairs:, :]
    return jnp.concatenate([below[:, :size], below[:, size:]], axis=0), ref[:pairs, :]


def store_packed(ref, left, right):
    pairs = ref.shape[1]
    half = left.shape[0] // 2
    ref[:pairs, :] = right
    ref[pairs:, : pairs // 2] = left[:half]
    ref[pairs:, pairs // 2 :] = left[half:]


def on_core(kernel, shapes, *operands, scalar=False):
    spaces = [pltpu.VMEM] * len(operands)
    if scalar:
        spaces[0] = pltpu.SMEM
    moved = sum(4 * operand.size for operand in operands)
    return pl.pallas_call(
        kernel,
        out_shape=shapes,
        in_specs=[whole(space) for space in spaces],
        out_specs=[whole(pltpu.VMEM)] * len(shapes),
        compiler_params=pltpu.CompilerParams(vmem_limit_bytes=VMEM_GRANT),
        cost_estimate=pl.CostEstimate(
            flops=256 * moved, bytes_accessed=2 * moved, transcendentals=0
        ),
    )(*operands)


def like(array):
    return jax.ShapeDtypeStruct(array.shape, jnp.float32)


def operators(rank, stacked, left_low, right_low):
    size, pairs = left_low.shape[0], right_low.shape[0]

    def kernel(rank_ref, stacked_ref, left_low_ref, right_low_ref, *outs):
        own_out, two_out, kept_out, block_out = outs
        rank = rank_ref[0]
        rows = lax.broadcasted_iota(jnp.int32, (size, size), 0)
        columns = lax.broadcasted_iota(jnp.int32, (size, size), 1)
        kept = jnp.logical_and(rows < rank, columns < rank)
        unit = jnp.where(rows == columns, 0.9, 0.0).astype(jnp.float32)
        left = jnp.where(kept, unit + stacked_ref[size + pairs :, :size], 0.0)
        left_before = jnp.where(kept, unit + left_low_ref[...], 0.0)
        rows = lax.broadcasted_iota(jnp.int32, (pairs, pairs), 0)
        columns = lax.broadcasted_iota(jnp.int32, (pairs, pairs), 1)
        unit = jnp.where(rows == columns, 0.9, 0.0).astype(jnp.float32)
        right = unit + stacked_ref[size : size + pairs, :]
        store_packed(own_out, left, right)
        left, right = times(left, left_before), times(unit + right_low_ref[...], right)
        store_packed(two_out, left, right)
        rows = lax.broadcasted_iota(jnp.int32, (size, pairs), 0)
        kept = jnp.where(rows < rank, stacked_ref[:size, :], 0.0)
        kept_out[...] = kept
        block_out[...] = absorb(left, kept, right)

    packed = jax.ShapeDtypeStruct((pairs + size // 2, pairs), jnp.float32)
    block = jax.ShapeDtypeStruct((size, pairs), jnp.float32)
    operands = rank, stacked, left_low, right_low
    return on_core(kernel, [packed, packed, block, block], *operands, scalar=True)


def joined(later, earlier):
    def kernel(later_ref, earlier_ref, out_ref):
        left, right = unpacked(later_ref)
        left_before, right_before = unpacked(earlier_ref)
        store_packed(out_ref, times(left, left_before), times(right_before, right))

    return on_core(kernel, [like(later)], later, earlier)[0]


def taken(operator, block, copies=1):
    def kernel(operator_ref, block_ref, *outs):
        left, right = unpacked(operator_ref)
        result = absorb(left, block_ref[...], right)
        for out_ref in outs:
            out_ref[...] = result

    return on_core(kernel, [like(block)] * copies, operator, block)


def last_rows(copies, operator, block, extra):
    rows, columns = block.shape

    def kernel(operator_ref, block_ref, extra_ref, block_out, outgoing_ref):
        left, right = unpacked(operator_ref)
        own = absorb(left, block_ref[...], right)
        block_out[...] = own
        rounded = own.astype(jnp.bfloat16)
        for index in range(copies):
            outgoing_ref[index, :rows, :] = rounded
            outgoing_ref[index, rows:, :] = extra_ref[...]

    outgoing = jax.ShapeDtypeStruct((copies, rows + EXTRA, columns), jnp.bfloat16)
    return on_core(kernel, [like(block), outgoing], operator, block, extra)


def environment_sums(slots, arrived, weights):
    sources, targets = slots.shape
    slot_count, inner, columns = weights.shape
    rows = arrived.shape[1] - EXTRA

    def kernel(slots_ref, arrived_ref, weights_ref, sums_ref):
        def one_target(target, carried):
            total = jnp.zeros((rows, columns), jnp.float32)
            for source in range(sources):
                slot = slots_ref[source, target]
                block = arrived_ref[source, :rows, :]
                block = jnp.where(slot >= 0, block, jnp.zeros_like(block))
                slot = jnp.minimum(jnp.maximum(slot, 0), slot_count - 1)
                total += jnp.dot(block, weights_ref[slot], preferred_element_type=jnp.float32)
            sums_ref[target] = total.astype(jnp.bfloat16)
            return carried

        for target in range(targets):
            one_target(target, 0)

    return pl.pallas_call(
        kernel,
        out_shape=jax.ShapeDtypeStruct((targets, rows, columns), jnp.bfloat16),
        in_specs=[whole(pltpu.SMEM), whole(pltpu.VMEM), whole(pltpu.VMEM)],
        out_specs=whole(pltpu.VMEM),
        compiler_params=pltpu.CompilerParams(vmem_limit_bytes=VMEM_GRANT),
        cost_estimate=pl.CostEstimate(
            flops=2 * sources * targets * rows * inner * columns,
            bytes_accessed=2 * (arrived.size + weights.size + targets * rows * columns),
            transcendentals=0,
        ),
    )(slots, arrived, weights)


def on_device(boundary_in, left_transfer, right_transfer, env_weight, ranks, routes, owner):
    block_size = boundary_in.shape[1]
    row_count = lax.axis_size("row")
    sector_count = lax.axis_size("sector")
    row = lax.axis_index("row")
    sector = lax.axis_index("sector")

    def sent(value, pairs):
        return lax.ppermute(value, "row", pairs)

    swap = [(r, r + 1) for r in range(0, row_count, 2)]
    right_low = sent(right_transfer[0], swap)
    left_low = sent(left_transfer[0, 0], swap)
    padded = jnp.pad(left_transfer[0, 0], ((0, 0), (0, boundary_in.shape[2] - block_size)))
    stacked = jnp.concatenate([boundary_in[0], right_transfer[0], padded], axis=0)
    own, two, initial, block = operators(ranks, stacked, left_low, right_low)
    arrived = sent(block, [(1, 3)])
    half = sent(two, [(r, r + 2) for r in range(5, row_count, 4)])

    last = row_count - 5
    source = jnp.where(row == 3, arrived, initial)
    (block,) = taken(two, arrived)
    leaving = block
    four = joined(two, half)
    hops = list(range(3, last, 4))
    for hop, start in enumerate(hops):
        arrived = sent(block, [(start, start + 4)])
        source = jnp.where(row == start + 4, arrived, source)
        end = hop == len(hops) - 1
        if end:
            spread = sent(leaving, [(r, r + 2) for r in hops])
            relayed = sent(half, [(r + 1, r) for r in range(6, row_count, 4)])
        block, *more = taken(four, arrived, copies=2 if end else 1)
        if not end:
            leaving = jnp.where(row == start + 4, block, leaving)
    for_end = sent(block, [(last, last + 3)])
    for_spread = sent(more[0], [(last, last + 1)])
    source = jnp.where((row % 4 == 1) & (row > 1), spread, source)
    arrived = sent(source, [(r + 1, r) for r in range(2, last, 2)])
    source = jnp.where((row % 2 == 0) & (row > 0), arrived, source)
    source = jnp.where(row == last + 3, for_end, source)
    source = jnp.where(row == last + 1, for_spread, source)
    arrived = sent(source, [(last + 1, last + 2), (last + 3, last + 4)])
    source = jnp.where((row == last + 2) | (row == last + 4), arrived, source)
    second = row % 2 == 1
    base = jnp.where(second, two, own)
    final = joined(base, jnp.where(second, half, relayed))
    final = jnp.where((row % 4 >= 2) & (row >= 4), final, base)

    along = ALONG
    across = sector_count // along
    parts = along // PAIR
    tiles = [
        [x * along + part * PAIR + y for x in TILE_ORDER for y in range(PAIR)]
        for part in range(parts)
    ]
    lines = [
        [x * along + part * PAIR + y for part in LINE_ORDER]
        for x in range(across)
        for y in range(PAIR)
    ]
    sector_ids = jnp.arange(sector_count)
    matches = (routes[0][:, None] == sector_ids[None, :]).astype(jnp.int32)
    target_owner = jnp.sum(matches * owner[None, :], axis=1)
    hits = (target_owner[:, None] == jnp.arange(block_size * 2)[None, :]).astype(jnp.int32)
    slot_of = jnp.sum(hits * (jnp.arange(routes.shape[1]) + 1)[:, None], axis=0)
    extra = jnp.broadcast_to(slot_of.astype(jnp.bfloat16), (EXTRA, block_size * 2))
    current, outgoing = last_rows(across * PAIR, final, source, extra)
    arrived = lax.all_to_all(
        outgoing,
        "sector", 0, 0, axis_index_groups=tiles, tiled=True,
    )
    targets = (sector // along) * along + sector % PAIR + jnp.asarray(LINE_ORDER) * PAIR
    wanted = (jnp.arange(block_size * 2)[None, :] == targets[:, None]).astype(jnp.float32)
    slots = jnp.sum(arrived[:, block_size, None, :].astype(jnp.float32) * wanted[None], axis=2)
    sums = environment_sums(slots.astype(jnp.int32) - 1, arrived, env_weight[0])
    terms = lax.all_to_all(sums, "sector", 0, 0, axis_index_groups=lines, tiled=True)
    environment = jnp.sum(terms.astype(jnp.float32), axis=0)
    return (current[None, None], environment[None, None])


def solution(mesh):
    return jax.shard_map(
        on_device,
        mesh=mesh,
        in_specs=(
            P("sector", None, None),
            P("row", "sector", None, None),
            P("row", None, None),
            P("row", None, None, None),
            P("sector"),
            P("sector", None),
            P(),
        ),
        out_specs=(P("row", "sector", None, None), P("row", "sector", None, None)),
        check_vma=False,
    )
```

```python
import jax
import jax.numpy as jnp
from jax import lax
from jax.experimental import pallas as pl
from jax.experimental.pallas import tpu as pltpu
from jax.sharding import PartitionSpec as P

ALONG = 8
PAIR = 2
EXTRA = 8
TILE_ORDER = (2, 3, 0, 1)
LINE_ORDER = (2, 3, 0, 1)
VMEM_GRANT = 8 * 1024 * 1024


def whole(space):
    return pl.BlockSpec(memory_space=space)


def times(a, b):
    def parts(value):
        head = value.astype(jnp.bfloat16)
        return head, (value - head.astype(jnp.float32)).astype(jnp.bfloat16)

    def dot(first, second):
        return jnp.dot(first, second, preferred_element_type=jnp.float32)

    (a_head, a_rest), (b_head, b_rest) = parts(a), parts(b)
    return dot(a_head, b_head) + (dot(a_head, b_rest) + dot(a_rest, b_head))


def absorb(left, block, right):
    return times(times(left, block), right)


def unpacked(ref):
    pairs = ref.shape[1]
    size = pairs // 2
    below = ref[pairs:, :]
    return jnp.concatenate([below[:, :size], below[:, size:]], axis=0), ref[:pairs, :]


def store_packed(ref, left, right):
    pairs = ref.shape[1]
    half = left.shape[0] // 2
    ref[:pairs, :] = right
    ref[pairs:, : pairs // 2] = left[:half]
    ref[pairs:, pairs // 2 :] = left[half:]


def on_core(kernel, shapes, *operands, scalar=False):
    spaces = [pltpu.VMEM] * len(operands)
    if scalar:
        spaces[0] = pltpu.SMEM
    moved = sum(4 * operand.size for operand in operands)
    return pl.pallas_call(
        kernel,
        out_shape=shapes,
        in_specs=[whole(space) for space in spaces],
        out_specs=[whole(pltpu.VMEM)] * len(shapes),
        compiler_params=pltpu.CompilerParams(vmem_limit_bytes=VMEM_GRANT),
        cost_estimate=pl.CostEstimate(
            flops=256 * moved, bytes_accessed=2 * moved, transcendentals=0
        ),
    )(*operands)


def like(array):
    return jax.ShapeDtypeStruct(array.shape, jnp.float32)


def operators(rank, stacked, left_low, right_low):
    size, pairs = left_low.shape[0], right_low.shape[0]

    def kernel(rank_ref, stacked_ref, left_low_ref, right_low_ref, *outs):
        own_out, two_out, kept_out, block_out = outs
        rank = rank_ref[0]
        rows = lax.broadcasted_iota(jnp.int32, (size, size), 0)
        columns = lax.broadcasted_iota(jnp.int32, (size, size), 1)
        kept = jnp.logical_and(rows < rank, columns < rank)
        unit = jnp.where(rows == columns, 0.9, 0.0).astype(jnp.float32)
        left = jnp.where(kept, unit + stacked_ref[size + pairs :, :size], 0.0)
        left_before = jnp.where(kept, unit + left_low_ref[...], 0.0)
        rows = lax.broadcasted_iota(jnp.int32, (pairs, pairs), 0)
        columns = lax.broadcasted_iota(jnp.int32, (pairs, pairs), 1)
        unit = jnp.where(rows == columns, 0.9, 0.0).astype(jnp.float32)
        right = unit + stacked_ref[size : size + pairs, :]
        store_packed(own_out, left, right)
        left, right = times(left, left_before), times(unit + right_low_ref[...], right)
        store_packed(two_out, left, right)
        rows = lax.broadcasted_iota(jnp.int32, (size, pairs), 0)
        kept = jnp.where(rows < rank, stacked_ref[:size, :], 0.0)
        kept_out[...] = kept
        block_out[...] = absorb(left, kept, right)

    packed = jax.ShapeDtypeStruct((pairs + size // 2, pairs), jnp.float32)
    block = jax.ShapeDtypeStruct((size, pairs), jnp.float32)
    operands = rank, stacked, left_low, right_low
    return on_core(kernel, [packed, packed, block, block], *operands, scalar=True)


def joined(later, earlier):
    def kernel(later_ref, earlier_ref, out_ref):
        left, right = unpacked(later_ref)
        left_before, right_before = unpacked(earlier_ref)
        store_packed(out_ref, times(left, left_before), times(right_before, right))

    return on_core(kernel, [like(later)], later, earlier)[0]


def taken(operator, block, copies=1):
    def kernel(operator_ref, block_ref, *outs):
        left, right = unpacked(operator_ref)
        result = absorb(left, block_ref[...], right)
        for out_ref in outs:
            out_ref[...] = result

    return on_core(kernel, [like(block)] * copies, operator, block)


def last_rows(copies, operator, block, extra):
    rows, columns = block.shape

    def kernel(operator_ref, block_ref, extra_ref, block_out, outgoing_ref):
        left, right = unpacked(operator_ref)
        own = absorb(left, block_ref[...], right)
        block_out[...] = own
        rounded = own.astype(jnp.bfloat16)
        for index in range(copies):
            outgoing_ref[index, :rows, :] = rounded
            outgoing_ref[index, rows:, :] = extra_ref[...]

    outgoing = jax.ShapeDtypeStruct((copies, rows + EXTRA, columns), jnp.bfloat16)
    return on_core(kernel, [like(block), outgoing], operator, block, extra)


def environment_sums(slots, arrived, weights):
    sources, targets = slots.shape
    slot_count, inner, columns = weights.shape
    rows = arrived.shape[1] - EXTRA

    def kernel(slots_ref, arrived_ref, weights_ref, sums_ref, total_ref):
        def one_target(target, carried):
            total_ref[target] = jnp.zeros((rows, columns), jnp.float32)
            for source in range(sources):
                slot = slots_ref[source, target]

                @pl.when(slot >= 0)
                def _add(source=source, slot=slot):
                    total_ref[target] += jnp.dot(
                        arrived_ref[source, :rows, :],
                        weights_ref[jnp.minimum(slot, slot_count - 1)],
                        preferred_element_type=jnp.float32,
                    )

            sums_ref[target] = total_ref[target].astype(jnp.bfloat16)
            return carried

        for target in range(targets):
            one_target(target, 0)

    return pl.pallas_call(
        kernel,
        out_shape=jax.ShapeDtypeStruct((targets, rows, columns), jnp.bfloat16),
        in_specs=[whole(pltpu.SMEM), whole(pltpu.VMEM), whole(pltpu.VMEM)],
        out_specs=whole(pltpu.VMEM),
        scratch_shapes=[pltpu.VMEM((targets, rows, columns), jnp.float32)],
        compiler_params=pltpu.CompilerParams(vmem_limit_bytes=VMEM_GRANT),
        cost_estimate=pl.CostEstimate(
            flops=2 * sources * targets * rows * inner * columns,
            bytes_accessed=2 * (arrived.size + weights.size + targets * rows * columns),
            transcendentals=0,
        ),
    )(slots, arrived, weights)


def on_device(boundary_in, left_transfer, right_transfer, env_weight, ranks, routes, owner):
    block_size = boundary_in.shape[1]
    row_count = lax.axis_size("row")
    sector_count = lax.axis_size("sector")
    row = lax.axis_index("row")
    sector = lax.axis_index("sector")

    def sent(value, pairs):
        return lax.ppermute(value, "row", pairs)

    swap = [(r, r + 1) for r in range(0, row_count, 2)]
    right_low = sent(right_transfer[0], swap)
    left_low = sent(left_transfer[0, 0], swap)
    padded = jnp.pad(left_transfer[0, 0], ((0, 0), (0, boundary_in.shape[2] - block_size)))
    stacked = jnp.concatenate([boundary_in[0], right_transfer[0], padded], axis=0)
    own, two, initial, block = operators(ranks, stacked, left_low, right_low)
    arrived = sent(block, [(1, 3)])
    half = sent(two, [(r, r + 2) for r in range(5, row_count, 4)])

    last = row_count - 5
    source = jnp.where(row == 3, arrived, initial)
    (block,) = taken(two, arrived)
    leaving = block
    four = joined(two, half)
    hops = list(range(3, last, 4))
    for hop, start in enumerate(hops):
        arrived = sent(block, [(start, start + 4)])
        source = jnp.where(row == start + 4, arrived, source)
        end = hop == len(hops) - 1
        if end:
            spread = sent(leaving, [(r, r + 2) for r in hops])
            relayed = sent(half, [(r + 1, r) for r in range(6, row_count, 4)])
        block, *more = taken(four, arrived, copies=2 if end else 1)
        if not end:
            leaving = jnp.where(row == start + 4, block, leaving)
    for_end = sent(block, [(last, last + 3)])
    for_spread = sent(more[0], [(last, last + 1)])
    source = jnp.where((row % 4 == 1) & (row > 1), spread, source)
    arrived = sent(source, [(r + 1, r) for r in range(2, last, 2)])
    source = jnp.where((row % 2 == 0) & (row > 0), arrived, source)
    source = jnp.where(row == last + 3, for_end, source)
    source = jnp.where(row == last + 1, for_spread, source)
    arrived = sent(source, [(last + 1, last + 2), (last + 3, last + 4)])
    source = jnp.where((row == last + 2) | (row == last + 4), arrived, source)
    second = row % 2 == 1
    base = jnp.where(second, two, own)
    final = joined(base, jnp.where(second, half, relayed))
    final = jnp.where((row % 4 >= 2) & (row >= 4), final, base)

    along = ALONG
    across = sector_count // along
    parts = along // PAIR
    tiles = [
        [x * along + part * PAIR + y for x in TILE_ORDER for y in range(PAIR)]
        for part in range(parts)
    ]
    lines = [
        [x * along + part * PAIR + y for part in LINE_ORDER]
        for x in range(across)
        for y in range(PAIR)
    ]
    sector_ids = jnp.arange(sector_count)
    matches = (routes[0][:, None] == sector_ids[None, :]).astype(jnp.int32)
    target_owner = jnp.sum(matches * owner[None, :], axis=1)
    hits = (target_owner[:, None] == jnp.arange(block_size * 2)[None, :]).astype(jnp.int32)
    slot_of = jnp.sum(hits * (jnp.arange(routes.shape[1]) + 1)[:, None], axis=0)
    extra = jnp.broadcast_to(slot_of.astype(jnp.bfloat16), (EXTRA, block_size * 2))
    current, outgoing = last_rows(across * PAIR, final, source, extra)
    arrived = lax.all_to_all(
        outgoing,
        "sector", 0, 0, axis_index_groups=tiles, tiled=True,
    )
    targets = (sector // along) * along + sector % PAIR + jnp.asarray(LINE_ORDER) * PAIR
    wanted = (jnp.arange(block_size * 2)[None, :] == targets[:, None]).astype(jnp.float32)
    slots = jnp.sum(arrived[:, block_size, None, :].astype(jnp.float32) * wanted[None], axis=2)
    sums = environment_sums(slots.astype(jnp.int32) - 1, arrived, env_weight[0])
    terms = lax.all_to_all(sums, "sector", 0, 0, axis_index_groups=lines, tiled=True)
    environment = jnp.sum(terms.astype(jnp.float32), axis=0)
    return (current[None, None], environment[None, None])


def solution(mesh):
    return jax.shard_map(
        on_device,
        mesh=mesh,
        in_specs=(
            P("sector", None, None),
            P("row", "sector", None, None),
            P("row", None, None),
            P("row", None, None, None),
            P("sector"),
            P("sector", None),
            P(),
        ),
        out_specs=(P("row", "sector", None, None), P("row", "sector", None, None)),
        check_vma=False,
    )
```
